512 devices in a mesh: pix: 64 (over z, y), train: 8 (over x, core).
Axes of the slice: x: 4, y: 4, z: 16, core: 2. Of those that a mesh axis runs over, the one named last changes fastest.
Arguments:
- raw_frames: bfloat16 [24, 352, 16384], P('train', None, 'pix'), may hold values from 60 to 160
- gain_section: int32 [24, 352, 16384], P('train', None, 'pix'), may hold values from 0 to 2
- dark_offset: bfloat16 [3, 352, 16384], P(None, None, 'pix'), may hold values from 0 to 40
- rel_gain: float32 [3, 16384], P(None, 'pix'), may hold values from 0.5 to 8
- cycle_label: int32 [16384, 1], P('pix'), may hold values from 0 to 191; in each aligned block of 256 rows (0 to 255, 256 to 511, ...) at most 2 rows name the same one
- cycle_slot: int32 [192], replicated, may hold values from 0 to 191, each once
Outputs:
- two_time: float32 [192, 352, 352], P('pix', 'train')
The draws below stay inside these ranges and needn't reach their ends.
Inputs may be any that keep to these rules, and one draw needn't show every extreme that they name: `cycle_label`: among the pixels of one index of pix no cycle holds more than 2 pixels; every cycle holds some pixel. `cycle_slot`: A permutation of the cycles.
All inputs are finite; a program needn't handle non-finite values.
Results may differ from the reference program's by a relative error of at most 0.0003.
Values sent between devices are 32-bit elements; how exact they have to be, the bound alone decides.
A program may use at most 64 MiB of HBM per device.

```python
import math
import jax
import jax.numpy as jnp
import numpy as np
from jax import lax

F = 352
GAINS = 3
P_DEV = 256
CYCLES = 192
PIXELS = 16384
TRAINS = 24
MOST = 2
N_PIX = 64


def touch_ends(entries, rng, least, largest):
    extent = entries.shape
    index_at = [jax.random.randint(jax.random.fold_in(rng, axis), (), 0, extent[axis]) for axis in range(len(extent))]
    entries = entries.at[tuple(index_at)].set(least)
    longest = extent.index(max(extent))
    index_at[longest] = (index_at[longest] + 1) % extent[longest]
    return entries.at[tuple(index_at)].set(largest)


def block_levels(stream_key, extent, pieces, least, largest):
    level, own = 1.0, jax.random.fold_in(stream_key, 6)
    for dim, parts in pieces:
        steps = jnp.exp(jax.random.uniform(jax.random.fold_in(own, dim), (parts,), jnp.float32, least / len(pieces), largest / len(pieces)))
        level = level * jnp.repeat(steps, extent[dim] // parts).reshape([-1 if axis == dim else 1 for axis in range(len(extent))])
    return level


def assign_block(own_key, own, number, rows, amount, top, most, lean):
    ranking = jax.random.permutation(own_key, amount)
    packed, common = portions_of(amount, rows * top, most, lean, True), portions_of(amount, rows * top, most, lean, False)
    places = jnp.arange(amount)

    def named(tallies, rotation):
        used = int((tallies > 0).sum())
        fixed = max(1, used // 4)
        shifted = fixed + (places - fixed + rotation * (used - fixed)) % max(1, amount - fixed)
        return jnp.zeros((amount,), jnp.int32).at[ranking[jnp.where(places < fixed, places, shifted)]].set(jnp.asarray(tallies, jnp.int32))

    tallies = jnp.where(number % 4 == 0, named(packed, number // 4), named(common, number - number // 4 - 1))
    mixed = jax.random.permutation(jax.random.fold_in(own, 3), amount)
    donor, receiver = mixed[0:amount // 2 * 2:2], mixed[1:amount // 2 * 2:2]
    margin = jnp.minimum(tallies[donor] - 1, most - tallies[receiver]) // 2
    margin = jnp.where((donor == ranking[0]) | (receiver == ranking[0]) | (tallies[receiver] == 0), 0, jnp.maximum(margin, 0))
    shifted = jax.random.randint(jax.random.fold_in(own, 4), (amount // 2,), 0, 1 << 20) % (margin + 1)
    tallies = tallies.at[donor].add(-shifted).at[receiver].add(shifted)
    items = jnp.searchsorted(jnp.cumsum(tallies), jnp.arange(rows * top), side="right").astype(jnp.int32)
    grid = items.reshape(top, rows).T
    grid = grid[jax.random.permutation(jax.random.fold_in(own, 1), rows)]
    rotation = jax.random.randint(jax.random.fold_in(own, 2), (rows, 1), 0, top)
    return jnp.take_along_axis(grid, (jnp.arange(top)[None, :] + rotation) % top, axis=1)


def portions_of(number_of, total, limit, slope, full):
    weights = [(1 << 20) // math.isqrt(grade ** slope) + 1 for grade in range(1, number_of + 1)]
    largest = limit if full else min(limit, max(-(-total // number_of), total * weights[0] // sum(weights)))
    least = 1 if total - largest >= number_of - 1 else 0
    counts, rest = [largest] + [least] * (number_of - 1), total - largest - least * (number_of - 1)
    while rest > 0:
        candidates = [i for i in range(1, number_of) if counts[i] < largest] or [i for i in range(1, number_of) if counts[i] < limit]
        pool, remaining = sum([weights[i] for i in candidates]), rest
        for i in candidates:
            extra = min(limit - counts[i], max(1, remaining * weights[i] // pool), rest)
            counts[i] = counts[i] + extra
            rest = rest - extra
    return np.array(counts)


def setup_inputs(seed: int = 0) -> dict:
    key_list = jax.random.split(jax.random.key(seed), 7)
    raw_frames = jnp.clip(60.0 + 100.0 * jax.random.uniform(key_list[0], (TRAINS, F, PIXELS), jnp.float32) ** block_levels(key_list[0], (TRAINS, F, PIXELS), ((0, 8), (2, 64)), -0.2, 0.2), 60.0, 160.0).astype(jnp.bfloat16)
    gain_section = touch_ends(jax.random.randint(key_list[1], (TRAINS, F, PIXELS), 0, 3), jax.random.fold_in(key_list[1], 1), 0, 2).astype(jnp.int32)
    dark_offset = jnp.clip(40.0 * jax.random.uniform(key_list[2], (GAINS, F, PIXELS), jnp.float32) ** block_levels(key_list[2], (GAINS, F, PIXELS), ((2, 64),), -0.2, 0.2), 0.0, 40.0).astype(jnp.bfloat16)
    rel_gain = jnp.clip(jnp.exp(math.log(8.0) - 2.7725887 * jax.random.uniform(key_list[3], (GAINS, PIXELS), jnp.float32) ** block_levels(key_list[3], (GAINS, PIXELS), ((1, 64),), -0.2, 0.2)), 0.5, 8.0)
    cycle_label_keys = jax.random.split(jax.random.fold_in(key_list[4], 1), PIXELS // P_DEV)
    cycle_label_turns = jax.random.permutation(jax.random.fold_in(key_list[4], 3), PIXELS // P_DEV)
    cycle_label = jax.vmap(lambda own, number: assign_block(jax.random.fold_in(key_list[4], 2), own, number, P_DEV, CYCLES, 1, MOST, 2))(cycle_label_keys, cycle_label_turns).reshape((PIXELS, 1))
    cycle_slot = jax.random.permutation(key_list[5], CYCLES).astype(jnp.int32)
    return {"raw_frames": raw_frames, "gain_section": gain_section, "dark_offset": dark_offset, "rel_gain": rel_gain, "cycle_label": cycle_label, "cycle_slot": cycle_slot}


def reference(raw_frames, gain_section, dark_offset, rel_gain, cycle_label, cycle_slot):
    labels = cycle_label[:, 0].astype(jnp.int32)
    slot_of = cycle_slot[labels].astype(jnp.int32)
    pixel_order = jnp.argsort(slot_of, stable=True).astype(jnp.int32)
    cycle_counts = jnp.zeros((CYCLES,), jnp.int32).at[slot_of].add(1).astype(jnp.int32)
    cycle_starts = (jnp.cumsum(cycle_counts) - cycle_counts).astype(jnp.int32)
    slot_width = N_PIX * MOST

    def per_cycle(which):
        column = jnp.arange(slot_width, dtype=jnp.int32)
        is_live = (column < cycle_counts[which]).astype(jnp.float32)
        where_at = jnp.minimum(cycle_starts[which] + column, PIXELS - 1).astype(jnp.int32)
        chosen = pixel_order[where_at]
        raw_part = raw_frames[:, :, chosen].astype(jnp.float32)
        section_part = gain_section[:, :, chosen]
        offset_part = dark_offset[:, :, chosen].astype(jnp.float32)
        gain_part = rel_gain[:, chosen]
        section_zero = section_part == 0
        section_one = section_part == 1
        offset = jnp.where(section_zero, offset_part[0], jnp.where(section_one, offset_part[1], offset_part[2]))
        factor = jnp.where(section_zero, gain_part[0], jnp.where(section_one, gain_part[1], gain_part[2]))
        intensity = (raw_part - offset) * factor * is_live
        gram_sum = jnp.einsum("tfw,tgw->fg", intensity, intensity, precision=lax.Precision.HIGHEST)
        frame_means = jnp.sum(intensity, axis=(0, 2))
        cycle_scale = TRAINS * cycle_counts[which].astype(jnp.float32)
        return cycle_scale * gram_sum / (frame_means[:, None] * frame_means[None, :])

    return lax.map(per_cycle, jnp.arange(CYCLES, dtype=jnp.int32))
```

```python
import jax
import jax.numpy as jnp
from jax import lax
from jax.sharding import PartitionSpec as P

CYCLE_DEV = 3
DEPTH = 2
BAND_PAD = 48


def slot_rows(raw_frames, gain_section, dark_offset, rel_gain, labels, slots, cycle_slot, bands):
    trains, pulses, pixels = raw_frames.shape
    section_zero = gain_section == 0
    section_one = gain_section == 1
    offset = jnp.where(
        section_zero, dark_offset[0], jnp.where(section_one, dark_offset[1], dark_offset[2])
    ).astype(jnp.float32)
    factor = jnp.where(section_zero, rel_gain[0], jnp.where(section_one, rel_gain[1], rel_gain[2]))
    intensity = (raw_frames.astype(jnp.float32) - offset) * factor
    band = pulses // bands
    grouped = intensity.reshape(trains, bands, band, pixels)
    ones = jnp.ones((trains, bands, 1, pixels), jnp.float32)
    zeros = jnp.zeros((trains, bands, BAND_PAD - band - 1, pixels), jnp.float32)
    grouped = jnp.concatenate([grouped, ones, zeros], axis=2).reshape(-1, pixels)
    cycle_count = cycle_slot.shape[0]
    member = labels[None, :] == jnp.arange(cycle_count, dtype=jnp.int32)[:, None]
    slot_of = jnp.sum(jnp.where(member, cycle_slot[:, None], 0), axis=0)
    index = jnp.arange(pixels, dtype=jnp.int32)
    earlier = (labels[:, None] == labels[None, :]) & (index[:, None] < index[None, :])
    within = jnp.sum(earlier.astype(jnp.int32), axis=0)
    position = slot_of * DEPTH + within
    chosen = (slots[:, None] == position[None, :]).astype(jnp.float32)
    return lax.dot_general(
        chosen, grouped, (((1,), (1,)), ((), ())), precision=lax.Precision.HIGHEST
    )


def normalise(total, band, bands):
    scale = total[:, band, band]
    rows_mean = total[:, :band, band]
    spread = total.reshape(total.shape[0], BAND_PAD, bands, BAND_PAD)[:, :, :, :band]
    spread = spread.reshape(total.shape[0], BAND_PAD, bands * band)
    return (
        scale[:, None, None]
        * spread[:, :band]
        / (rows_mean[:, :, None] * spread[:, band : band + 1, :])
    )


def on_device(raw_frames, gain_section, dark_offset, rel_gain, cycle_label, cycle_slot):
    trains, pulses, pixels = raw_frames.shape
    owners = lax.axis_size("pix")
    bands = lax.axis_size("train")
    cycle_count = cycle_slot.shape[0]
    slots = jnp.arange(cycle_count * DEPTH, dtype=jnp.int32)
    rows = slot_rows(
        raw_frames, gain_section, dark_offset, rel_gain, cycle_label[:, 0], slots, cycle_slot, bands
    )
    rows = rows.reshape(owners, CYCLE_DEV, DEPTH, -1)
    rows = lax.all_to_all(rows, "pix", split_axis=0, concat_axis=0, tiled=True)
    blocks = rows.reshape(owners, CYCLE_DEV, DEPTH, trains, bands * BAND_PAD)
    gram = jnp.einsum("okstf,okstg->kfg", blocks, blocks, precision=lax.Precision.HIGHEST)
    gram = gram.reshape(CYCLE_DEV, bands, BAND_PAD, bands * BAND_PAD)
    total = lax.psum_scatter(gram, "train", scatter_dimension=1, tiled=True)[:, 0]
    return normalise(total, pulses // bands, bands)


def solution(mesh):
    placed = (
        P("train", None, "pix"),
        P("train", None, "pix"),
        P(None, None, "pix"),
        P(None, "pix"),
        P("pix", None),
        P(),
    )
    return jax.shard_map(
        on_device, mesh=mesh, in_specs=placed, out_specs=P("pix", "train", None), check_vma=False
    )
```

```python
import functools

import jax
import jax.numpy as jnp
from jax import lax
from jax.experimental import pallas as pl
from jax.experimental.pallas import tpu as pltpu
from jax.sharding import PartitionSpec as P

CYCLE_DEV = 3
DEPTH = 2
BAND_PAD = 48
LANES = 128
TILES = 3
BANDS = 8
ROWS = 8
Y = 4
Z = 16
HALF = Z // 2
PEERS = Y * BANDS
LAG = 3
BLOCKS = [(b, j) for b in range(BANDS) for j in range(BAND_PAD * b // LANES, TILES)]
PER_CYCLE = len(BLOCKS)
PIECES = PER_CYCLE * CYCLE_DEV
MESH = pl.DeviceIdType.MESH


def kernel(
    send, out, recv, gram, up_buf, dn_buf, full, fin,
    own_sem, swap_send, swap_recv, up_send, dn_send, up_recv, dn_recv, fin_send, fin_recv,
):
    pix = lax.axis_index("pix")
    t = lax.axis_index("train")
    z, y = pix // Y, pix % Y
    me = y * BANDS + t
    turn = (z - t + Z) % Z
    s = turn % HALF
    far = jnp.where(turn < HALF, 1, 0)
    near = 1 - far
    above = {"pix": ((z + 1) % Z) * Y + y, "train": t}
    below = {"pix": ((z + Z - 1) % Z) * Y + y, "train": t}

    def peer(d):
        return {"pix": z * Y + d // BANDS, "train": d % BANDS}

    barrier = pltpu.get_barrier_semaphore()

    @pl.loop(1, PEERS)
    def _(i):
        pl.semaphore_signal(barrier, inc=1, device_id=peer((me + i) % PEERS), device_id_type=MESH)

    pl.semaphore_signal(barrier, inc=1, device_id=above, device_id_type=MESH)
    pl.semaphore_signal(barrier, inc=1, device_id=below, device_id_type=MESH)
    pl.semaphore_wait(barrier, PEERS + 1)

    for m in range(CYCLE_DEV):

        @pl.loop(1, PEERS)
        def _(i):
            d = (me + i) % PEERS
            pltpu.make_async_remote_copy(
                src_ref=send.at[m, d], dst_ref=recv.at[m, me],
                send_sem=swap_send.at[m], recv_sem=swap_recv.at[m],
                device_id=peer(d), device_id_type=MESH,
            ).start()

        pltpu.make_async_copy(send.at[m, me], recv.at[m, me], own_sem.at[m]).start()

    @pl.loop(0, CYCLE_DEV)
    def _(m):
        pltpu.make_async_copy(send.at[m, me], recv.at[m, me], own_sem.at[m]).wait()
        others = recv.at[m, pl.ds(0, PEERS - 1)]
        pltpu.make_async_copy(others, others, swap_recv.at[m]).wait()
        for h in range(2):
            rows = recv[m, :, h].reshape(PEERS * ROWS, TILES * LANES)
            head = rows.astype(jnp.bfloat16)
            tail = (rows - head.astype(jnp.float32)).astype(jnp.bfloat16)
            turned = rows.T
            head_t = turned.astype(jnp.bfloat16)
            tail_t = (turned - head_t.astype(jnp.float32)).astype(jnp.bfloat16)
            for j in range(TILES):
                bands = [b for b in range(BANDS) if BAND_PAD * b // LANES == j]
                low, high = bands[0] * BAND_PAD, (bands[-1] + 1) * BAND_PAD
                dot = functools.partial(jnp.dot, preferred_element_type=jnp.float32)
                right, right_tail = head[:, j * LANES :], tail[:, j * LANES :]
                part = (
                    dot(head_t[low:high], right)
                    + dot(head_t[low:high], right_tail)
                    + dot(tail_t[low:high], right)
                )
                for b in bands:
                    for jj in range(j, TILES):
                        gram[h, m * PER_CYCLE + BLOCKS.index((b, jj))] = part[
                            b * BAND_PAD - low : (b + 1) * BAND_PAD - low,
                            (jj - j) * LANES : (jj - j + 1) * LANES,
                        ]

    def up_copy(p):
        return pltpu.make_async_remote_copy(
            src_ref=gram.at[far, p], dst_ref=up_buf.at[p], send_sem=up_send, recv_sem=up_recv.at[p],
            device_id=above, device_id_type=MESH,
        )

    def dn_copy(p):
        return pltpu.make_async_remote_copy(
            src_ref=gram.at[near, p], dst_ref=dn_buf.at[p], send_sem=dn_send, recv_sem=dn_recv.at[p],
            device_id=below, device_id_type=MESH,
        )

    def hand_out(m, b):
        return pltpu.make_async_remote_copy(
            src_ref=full.at[m, b], dst_ref=fin.at[m], send_sem=fin_send.at[m], recv_sem=fin_recv.at[m],
            device_id={"pix": pix, "train": b}, device_id_type=MESH,
        )

    up_lag = s * LAG
    dn_lag = jnp.where(s == 0, HALF * LAG, (HALF - 1 - s) * LAG)

    @pl.loop(0, PIECES + HALF * LAG)
    def _(step):
        p = step - up_lag

        @pl.when((p >= 0) & (p < PIECES))
        def _():
            @pl.when(s > 0)
            def _():
                up_copy(p).wait_recv()
                gram[far, p] = gram[far, p] + up_buf[p]

            up_copy(p).start()

        q = step - dn_lag

        @pl.when((q >= 0) & (q < PIECES))
        def _():
            @pl.when(s > 0)
            def _():
                @pl.when(s < HALF - 1)
                def _():
                    dn_copy(q).wait_recv()
                    gram[near, q] = gram[near, q] + dn_buf[q]

                dn_copy(q).start()

            @pl.when(s == 0)
            def _():
                up_copy(q).wait_recv()
                dn_copy(q).wait_recv()
                gram[near, q] = gram[near, q] + (up_buf[q] + dn_buf[q])

                @pl.when(q % PER_CYCLE == PER_CYCLE - 1)
                def _():
                    m = q // PER_CYCLE

                    def block(b, j):
                        return gram[near, m * PER_CYCLE + BLOCKS.index((b, j))]

                    for b, j in BLOCKS:
                        full[m, b, j] = block(b, j)
                    first = jnp.concatenate(
                        [
                            jnp.concatenate([block(0, j), block(1, j), block(2, j)[:32]], 0).T
                            for j in (1, 2)
                        ],
                        0,
                    )
                    for b in range(3, BANDS):
                        full[m, b, 0] = first[b * BAND_PAD - LANES : (b + 1) * BAND_PAD - LANES]
                    second = jnp.concatenate(
                        [block(2, 2)[32:], block(3, 2), block(4, 2), block(5, 2)[:16]], 0
                    ).T
                    for b in range(6, BANDS):
                        low = b * BAND_PAD - 2 * LANES
                        full[m, b, 1] = second[low : low + BAND_PAD]

                    @pl.loop(1, BANDS)
                    def _(i):
                        hand_out(m, (t + i) % BANDS).start()

    @pl.loop(0, CYCLE_DEV)
    def _(m):
        @pl.when(s > 0)
        def _():
            hand_out(m, 0).wait_recv()
            for j in range(TILES):
                out[m, :, j * LANES : (j + 1) * LANES] = fin[m, j]

        @pl.when(s == 0)
        def _():
            for j in range(TILES):
                out[m, :, j * LANES : (j + 1) * LANES] = full[m, t, j]
            sent = full.at[m, pl.ds(0, BANDS - 1)]
            pltpu.make_async_copy(sent, sent, fin_send.at[m]).wait()

        others = send.at[m, pl.ds(0, PEERS - 1)]
        pltpu.make_async_copy(others, others, swap_send.at[m]).wait()

    pltpu.make_async_copy(up_buf, up_buf, up_send).wait()

    @pl.when(s > 0)
    def _():
        pltpu.make_async_copy(dn_buf, dn_buf, dn_send).wait()


def summed_bands(send):
    piece = (BAND_PAD, LANES)
    return pl.pallas_call(
        kernel,
        out_shape=jax.ShapeDtypeStruct((CYCLE_DEV, BAND_PAD, TILES * LANES), jnp.float32),
        in_specs=[pl.BlockSpec(memory_space=pltpu.VMEM)],
        out_specs=pl.BlockSpec(memory_space=pltpu.VMEM),
        scratch_shapes=[
            pltpu.VMEM((CYCLE_DEV, PEERS, 2, ROWS, TILES * LANES), jnp.float32),
            pltpu.VMEM((2, PIECES) + piece, jnp.float32),
            pltpu.VMEM((PIECES,) + piece, jnp.float32),
            pltpu.VMEM((PIECES,) + piece, jnp.float32),
            pltpu.VMEM((CYCLE_DEV, BANDS, TILES) + piece, jnp.float32),
            pltpu.VMEM((CYCLE_DEV, TILES) + piece, jnp.float32),
            pltpu.SemaphoreType.DMA((CYCLE_DEV,)),
            pltpu.SemaphoreType.DMA((CYCLE_DEV,)),
            pltpu.SemaphoreType.DMA((CYCLE_DEV,)),
            pltpu.SemaphoreType.DMA,
            pltpu.SemaphoreType.DMA,
            pltpu.SemaphoreType.DMA((PIECES,)),
            pltpu.SemaphoreType.DMA((PIECES,)),
            pltpu.SemaphoreType.DMA((CYCLE_DEV,)),
            pltpu.SemaphoreType.DMA((CYCLE_DEV,)),
        ],
        compiler_params=pltpu.CompilerParams(collective_id=0, has_side_effects=True),
        name="plane_gram",
    )(send)


def slot_rows(raw_frames, gain_section, dark_offset, rel_gain, labels, slots, cycle_slot, bands):
    trains, pulses, pixels = raw_frames.shape
    section_zero = gain_section == 0
    section_one = gain_section == 1
    offset = jnp.where(
        section_zero, dark_offset[0], jnp.where(section_one, dark_offset[1], dark_offset[2])
    ).astype(jnp.float32)
    factor = jnp.where(section_zero, rel_gain[0], jnp.where(section_one, rel_gain[1], rel_gain[2]))
    intensity = (raw_frames.astype(jnp.float32) - offset) * factor
    band = pulses // bands
    grouped = intensity.reshape(trains, bands, band, pixels)
    ones = jnp.ones((trains, bands, 1, pixels), jnp.float32)
    zeros = jnp.zeros((trains, bands, BAND_PAD - band - 1, pixels), jnp.float32)
    grouped = jnp.concatenate([grouped, ones, zeros], axis=2).reshape(-1, pixels)
    cycle_count = cycle_slot.shape[0]
    member = labels[None, :] == jnp.arange(cycle_count, dtype=jnp.int32)[:, None]
    slot_of = jnp.sum(jnp.where(member, cycle_slot[:, None], 0), axis=0)
    index = jnp.arange(pixels, dtype=jnp.int32)
    earlier = (labels[:, None] == labels[None, :]) & (index[:, None] < index[None, :])
    within = jnp.sum(earlier.astype(jnp.int32), axis=0)
    position = slot_of * DEPTH + within
    chosen = (slots[:, None] == position[None, :]).astype(jnp.float32)
    return lax.dot_general(
        chosen, grouped, (((1,), (1,)), ((), ())), precision=lax.Precision.HIGHEST
    )


def normalise(total, band, bands):
    scale = total[:, band, band]
    rows_mean = total[:, :band, band]
    spread = total.reshape(total.shape[0], BAND_PAD, bands, BAND_PAD)[:, :, :, :band]
    spread = spread.reshape(total.shape[0], BAND_PAD, bands * band)
    return (
        scale[:, None, None]
        * spread[:, :band]
        / (rows_mean[:, :, None] * spread[:, band : band + 1, :])
    )


def on_device(raw_frames, gain_section, dark_offset, rel_gain, cycle_label, cycle_slot):
    trains, pulses, pixels = raw_frames.shape
    order = jnp.arange(CYCLE_DEV * Z * Y, dtype=jnp.int32)
    m, rest = order // (PEERS * 2), order % (PEERS * 2)
    peer, half = rest // 2, rest % 2
    owner = (half * HALF + peer % BANDS) * Y + peer // BANDS
    slots = (owner * CYCLE_DEV + m)[:, None] * DEPTH + jnp.arange(DEPTH, dtype=jnp.int32)[None, :]
    rows = slot_rows(
        raw_frames, gain_section, dark_offset, rel_gain, cycle_label[:, 0], slots.reshape(-1),
        cycle_slot, BANDS,
    )
    rows = rows.reshape(CYCLE_DEV, PEERS, 2, DEPTH * trains, TILES * LANES)
    rows = jnp.pad(rows, ((0, 0), (0, 0), (0, 0), (0, ROWS - DEPTH * trains), (0, 0)))
    return normalise(summed_bands(rows), pulses // BANDS, BANDS)


def solution(mesh):
    placed = (
        P("train", None, "pix"),
        P("train", None, "pix"),
        P(None, None, "pix"),
        P(None, "pix"),
        P("pix", None),
        P(),
    )
    return jax.shard_map(
        on_device, mesh=mesh, in_specs=placed, out_specs=P("pix", "train", None), check_vma=False
    )
```

```python
import functools

import jax
import jax.numpy as jnp
from jax import lax
from jax.experimental import pallas as pl
from jax.experimental.pallas import tpu as pltpu
from jax.sharding import PartitionSpec as P

CYCLE_DEV = 3
DEPTH = 2
BAND_PAD = 48
LANES = 128
TILES = 3
BANDS = 8
ROWS = 8
Y = 4
Z = 16
HALF = Z // 2
PEERS = Y * BANDS
LAG = 7
BLOCKS = [(b, j) for b in range(BANDS) for j in range(BAND_PAD * b // LANES, TILES)]
PER_CYCLE = len(BLOCKS)
PIECES = PER_CYCLE * CYCLE_DEV
MESH = pl.DeviceIdType.MESH


def kernel(
    send, out, recv, gram, up_buf, dn_buf, full, fin,
    own_sem, swap_send, swap_recv, up_send, dn_send, up_recv, dn_recv, fin_send, fin_recv,
):
    pix = lax.axis_index("pix")
    t = lax.axis_index("train")
    z, y = pix // Y, pix % Y
    me = y * BANDS + t
    turn = (z - t + Z) % Z
    s = turn % HALF
    far = jnp.where(turn < HALF, 1, 0)
    near = 1 - far
    above = {"pix": ((z + 1) % Z) * Y + y, "train": t}
    below = {"pix": ((z + Z - 1) % Z) * Y + y, "train": t}

    def peer(d):
        return {"pix": z * Y + d // BANDS, "train": d % BANDS}

    barrier = pltpu.get_barrier_semaphore()

    @pl.loop(1, PEERS)
    def _(i):
        pl.semaphore_signal(barrier, inc=1, device_id=peer((me + i) % PEERS), device_id_type=MESH)

    pl.semaphore_signal(barrier, inc=1, device_id=above, device_id_type=MESH)
    pl.semaphore_signal(barrier, inc=1, device_id=below, device_id_type=MESH)
    pl.semaphore_wait(barrier, PEERS + 1)

    for m in range(CYCLE_DEV):

        @pl.loop(1, PEERS)
        def _(i):
            d = (me + i) % PEERS
            pltpu.make_async_remote_copy(
                src_ref=send.at[m, d], dst_ref=recv.at[m, me],
                send_sem=swap_send.at[m], recv_sem=swap_recv.at[m],
                device_id=peer(d), device_id_type=MESH,
            ).start()

        pltpu.make_async_copy(send.at[m, me], recv.at[m, me], own_sem.at[m]).start()

    def partial_grams(m):
        pltpu.make_async_copy(send.at[m, me], recv.at[m, me], own_sem.at[m]).wait()
        others = recv.at[m, pl.ds(0, PEERS - 1)]
        pltpu.make_async_copy(others, others, swap_recv.at[m]).wait()
        for h in range(2):
            rows = recv[m, :, h].reshape(PEERS * ROWS, TILES * LANES)
            head = rows.astype(jnp.bfloat16)
            tail = (rows - head.astype(jnp.float32)).astype(jnp.bfloat16)
            turned = rows.T
            head_t = turned.astype(jnp.bfloat16)
            tail_t = (turned - head_t.astype(jnp.float32)).astype(jnp.bfloat16)
            for j in range(TILES):
                bands = [b for b in range(BANDS) if BAND_PAD * b // LANES == j]
                low, high = bands[0] * BAND_PAD, (bands[-1] + 1) * BAND_PAD
                dot = functools.partial(jnp.dot, preferred_element_type=jnp.float32)
                right, right_tail = head[:, j * LANES :], tail[:, j * LANES :]
                part = (
                    dot(head_t[low:high], right)
                    + dot(head_t[low:high], right_tail)
                    + dot(tail_t[low:high], right)
                )
                for b in bands:
                    for jj in range(j, TILES):
                        gram[h, m * PER_CYCLE + BLOCKS.index((b, jj))] = part[
                            b * BAND_PAD - low : (b + 1) * BAND_PAD - low,
                            (jj - j) * LANES : (jj - j + 1) * LANES,
                        ]

    def up_copy(p):
        return pltpu.make_async_remote_copy(
            src_ref=gram.at[far, p], dst_ref=up_buf.at[p], send_sem=up_send, recv_sem=up_recv.at[p],
            device_id=above, device_id_type=MESH,
        )

    def dn_copy(p):
        return pltpu.make_async_remote_copy(
            src_ref=gram.at[near, p], dst_ref=dn_buf.at[p], send_sem=dn_send, recv_sem=dn_recv.at[p],
            device_id=below, device_id_type=MESH,
        )

    def hand_out(m, b):
        return pltpu.make_async_remote_copy(
            src_ref=full.at[m, b], dst_ref=fin.at[m], send_sem=fin_send.at[m], recv_sem=fin_recv.at[m],
            device_id={"pix": pix, "train": b}, device_id_type=MESH,
        )

    up_lag = s * LAG
    dn_lag = jnp.where(s == 0, HALF * LAG, (HALF - 1 - s) * LAG)

    def advance(step):
        p = step - up_lag

        @pl.when((p >= 0) & (p < PIECES))
        def _():
            @pl.when(s > 0)
            def _():
                up_copy(p).wait_recv()
                gram[far, p] = gram[far, p] + up_buf[p]

            up_copy(p).start()

        q = step - dn_lag

        @pl.when((q >= 0) & (q < PIECES))
        def _():
            @pl.when(s > 0)
            def _():
                @pl.when(s < HALF - 1)
                def _():
                    dn_copy(q).wait_recv()
                    gram[near, q] = gram[near, q] + dn_buf[q]

                dn_copy(q).start()

            @pl.when(s == 0)
            def _():
                up_copy(q).wait_recv()
                dn_copy(q).wait_recv()
                gram[near, q] = gram[near, q] + (up_buf[q] + dn_buf[q])

                @pl.when(q % PER_CYCLE == PER_CYCLE - 1)
                def _():
                    m = q // PER_CYCLE

                    def block(b, j):
                        return gram[near, m * PER_CYCLE + BLOCKS.index((b, j))]

                    for b, j in BLOCKS:
                        full[m, b, j] = block(b, j)
                    first = jnp.concatenate(
                        [
                            jnp.concatenate([block(0, j), block(1, j), block(2, j)[:32]], 0).T
                            for j in (1, 2)
                        ],
                        0,
                    )
                    for b in range(3, BANDS):
                        full[m, b, 0] = first[b * BAND_PAD - LANES : (b + 1) * BAND_PAD - LANES]
                    second = jnp.concatenate(
                        [block(2, 2)[32:], block(3, 2), block(4, 2), block(5, 2)[:16]], 0
                    ).T
                    for b in range(6, BANDS):
                        low = b * BAND_PAD - 2 * LANES
                        full[m, b, 1] = second[low : low + BAND_PAD]

                    @pl.loop(1, BANDS)
                    def _(i):
                        hand_out(m, (t + i) % BANDS).start()

    @pl.loop(0, CYCLE_DEV)
    def _(m):
        partial_grams(m)

        @pl.loop(m * PER_CYCLE, (m + 1) * PER_CYCLE)
        def _(step):
            advance(step)

    @pl.loop(PIECES, PIECES + HALF * LAG)
    def _(step):
        advance(step)

    @pl.loop(0, CYCLE_DEV)
    def _(m):
        @pl.when(s > 0)
        def _():
            hand_out(m, 0).wait_recv()
            for j in range(TILES):
                out[m, :, j * LANES : (j + 1) * LANES] = fin[m, j]

        @pl.when(s == 0)
        def _():
            for j in range(TILES):
                out[m, :, j * LANES : (j + 1) * LANES] = full[m, t, j]
            sent = full.at[m, pl.ds(0, BANDS - 1)]
            pltpu.make_async_copy(sent, sent, fin_send.at[m]).wait()

        others = send.at[m, pl.ds(0, PEERS - 1)]
        pltpu.make_async_copy(others, others, swap_send.at[m]).wait()

    pltpu.make_async_copy(up_buf, up_buf, up_send).wait()

    @pl.when(s > 0)
    def _():
        pltpu.make_async_copy(dn_buf, dn_buf, dn_send).wait()


def summed_bands(send):
    piece = (BAND_PAD, LANES)
    return pl.pallas_call(
        kernel,
        out_shape=jax.ShapeDtypeStruct((CYCLE_DEV, BAND_PAD, TILES * LANES), jnp.float32),
        in_specs=[pl.BlockSpec(memory_space=pltpu.VMEM)],
        out_specs=pl.BlockSpec(memory_space=pltpu.VMEM),
        scratch_shapes=[
            pltpu.VMEM((CYCLE_DEV, PEERS, 2, ROWS, TILES * LANES), jnp.float32),
            pltpu.VMEM((2, PIECES) + piece, jnp.float32),
            pltpu.VMEM((PIECES,) + piece, jnp.float32),
            pltpu.VMEM((PIECES,) + piece, jnp.float32),
            pltpu.VMEM((CYCLE_DEV, BANDS, TILES) + piece, jnp.float32),
            pltpu.VMEM((CYCLE_DEV, TILES) + piece, jnp.float32),
            pltpu.SemaphoreType.DMA((CYCLE_DEV,)),
            pltpu.SemaphoreType.DMA((CYCLE_DEV,)),
            pltpu.SemaphoreType.DMA((CYCLE_DEV,)),
            pltpu.SemaphoreType.DMA,
            pltpu.SemaphoreType.DMA,
            pltpu.SemaphoreType.DMA((PIECES,)),
            pltpu.SemaphoreType.DMA((PIECES,)),
            pltpu.SemaphoreType.DMA((CYCLE_DEV,)),
            pltpu.SemaphoreType.DMA((CYCLE_DEV,)),
        ],
        compiler_params=pltpu.CompilerParams(collective_id=0, has_side_effects=True),
        name="plane_gram",
    )(send)


def slot_rows(raw_frames, gain_section, dark_offset, rel_gain, labels, slots, cycle_slot, bands):
    trains, pulses, pixels = raw_frames.shape
    section_zero = gain_section == 0
    section_one = gain_section == 1
    offset = jnp.where(
        section_zero, dark_offset[0], jnp.where(section_one, dark_offset[1], dark_offset[2])
    ).astype(jnp.float32)
    factor = jnp.where(section_zero, rel_gain[0], jnp.where(section_one, rel_gain[1], rel_gain[2]))
    intensity = (raw_frames.astype(jnp.float32) - offset) * factor
    band = pulses // bands
    grouped = intensity.reshape(trains, bands, band, pixels)
    ones = jnp.ones((trains, bands, 1, pixels), jnp.float32)
    zeros = jnp.zeros((trains, bands, BAND_PAD - band - 1, pixels), jnp.float32)
    grouped = jnp.concatenate([grouped, ones, zeros], axis=2).reshape(-1, pixels)
    cycle_count = cycle_slot.shape[0]
    member = labels[None, :] == jnp.arange(cycle_count, dtype=jnp.int32)[:, None]
    slot_of = jnp.sum(jnp.where(member, cycle_slot[:, None], 0), axis=0)
    index = jnp.arange(pixels, dtype=jnp.int32)
    earlier = (labels[:, None] == labels[None, :]) & (index[:, None] < index[None, :])
    within = jnp.sum(earlier.astype(jnp.int32), axis=0)
    position = slot_of * DEPTH + within
    chosen = (slots[:, None] == position[None, :]).astype(jnp.float32)
    return lax.dot_general(
        chosen, grouped, (((1,), (1,)), ((), ())), precision=lax.Precision.HIGHEST
    )


def normalise(total, band, bands):
    scale = total[:, band, band]
    rows_mean = total[:, :band, band]
    spread = total.reshape(total.shape[0], BAND_PAD, bands, BAND_PAD)[:, :, :, :band]
    spread = spread.reshape(total.shape[0], BAND_PAD, bands * band)
    return (
        scale[:, None, None]
        * spread[:, :band]
        / (rows_mean[:, :, None] * spread[:, band : band + 1, :])
    )


def on_device(raw_frames, gain_section, dark_offset, rel_gain, cycle_label, cycle_slot):
    trains, pulses, pixels = raw_frames.shape
    order = jnp.arange(CYCLE_DEV * Z * Y, dtype=jnp.int32)
    m, rest = order // (PEERS * 2), order % (PEERS * 2)
    peer, half = rest // 2, rest % 2
    owner = (half * HALF + peer % BANDS) * Y + peer // BANDS
    slots = (owner * CYCLE_DEV + m)[:, None] * DEPTH + jnp.arange(DEPTH, dtype=jnp.int32)[None, :]
    rows = slot_rows(
        raw_frames, gain_section, dark_offset, rel_gain, cycle_label[:, 0], slots.reshape(-1),
        cycle_slot, BANDS,
    )
    rows = rows.reshape(CYCLE_DEV, PEERS, 2, DEPTH * trains, TILES * LANES)
    rows = jnp.pad(rows, ((0, 0), (0, 0), (0, 0), (0, ROWS - DEPTH * trains), (0, 0)))
    return normalise(summed_bands(rows), pulses // BANDS, BANDS)


def solution(mesh):
    placed = (
        P("train", None, "pix"),
        P("train", None, "pix"),
        P(None, None, "pix"),
        P(None, "pix"),
        P("pix", None),
        P(),
    )
    return jax.shard_map(
        on_device, mesh=mesh, in_specs=placed, out_specs=P("pix", "train", None), check_vma=False
    )
```

```python
import functools

import jax
import jax.numpy as jnp
from jax import lax
from jax.experimental import pallas as pl
from jax.experimental.pallas import tpu as pltpu
from jax.sharding import PartitionSpec as P

CYCLE_DEV = 3
DEPTH = 2
BAND_PAD = 48
LANES = 128
TILES = 3
BANDS = 8
ROWS = 8
Y = 4
Z = 16
HALF = Z // 2
PEERS = Y * BANDS
LAG = 7
BLOCKS = [(b, j) for b in range(BANDS) for j in range(BAND_PAD * b // LANES, TILES)]
PER_CYCLE = len(BLOCKS)
PIECES = PER_CYCLE * CYCLE_DEV
MESH = pl.DeviceIdType.MESH


def kernel(
    send, out, recv, gram, up_buf, dn_buf, full, fin,
    own_sem, swap_send, swap_recv, up_send, dn_send, up_recv, dn_recv, fin_send, fin_recv,
):
    pix = lax.axis_index("pix")
    t = lax.axis_index("train")
    z, y = pix // Y, pix % Y
    me = y * BANDS + t
    turn = (z - t + Z) % Z
    s = turn % HALF
    far = jnp.where(turn < HALF, 1, 0)
    near = 1 - far
    above = {"pix": ((z + 1) % Z) * Y + y, "train": t}
    below = {"pix": ((z + Z - 1) % Z) * Y + y, "train": t}

    def peer(d):
        return {"pix": z * Y + d // BANDS, "train": d % BANDS}

    barrier = pltpu.get_barrier_semaphore()

    @pl.loop(1, PEERS)
    def _(i):
        pl.semaphore_signal(barrier, inc=1, device_id=peer((me + i) % PEERS), device_id_type=MESH)

    pl.semaphore_signal(barrier, inc=1, device_id=above, device_id_type=MESH)
    pl.semaphore_signal(barrier, inc=1, device_id=below, device_id_type=MESH)
    pl.semaphore_wait(barrier, PEERS + 1)

    for m in range(CYCLE_DEV):

        @pl.loop(1, PEERS)
        def _(i):
            d = (me + i) % PEERS
            pltpu.make_async_remote_copy(
                src_ref=send.at[m, d], dst_ref=recv.at[m, me],
                send_sem=swap_send.at[m], recv_sem=swap_recv.at[m],
                device_id=peer(d), device_id_type=MESH,
            ).start()

        pltpu.make_async_copy(send.at[m, me], recv.at[m, me], own_sem.at[m]).start()

    def partial_grams(m):
        pltpu.make_async_copy(send.at[m, me], recv.at[m, me], own_sem.at[m]).wait()
        others = recv.at[m, pl.ds(0, PEERS - 1)]
        pltpu.make_async_copy(others, others, swap_recv.at[m]).wait()
        for h in range(2):
            rows = recv[m, :, h].reshape(PEERS * ROWS, TILES * LANES)
            head = rows.astype(jnp.bfloat16)
            tail = (rows - head.astype(jnp.float32)).astype(jnp.bfloat16)
            turned = rows.T
            head_t = turned.astype(jnp.bfloat16)
            tail_t = (turned - head_t.astype(jnp.float32)).astype(jnp.bfloat16)
            for j in range(TILES):
                bands = [b for b in range(BANDS) if BAND_PAD * b // LANES == j]
                low, high = bands[0] * BAND_PAD, (bands[-1] + 1) * BAND_PAD
                dot = functools.partial(jnp.dot, preferred_element_type=jnp.float32)
                right, right_tail = head[:, j * LANES :], tail[:, j * LANES :]
                part = (
                    dot(head_t[low:high], right)
                    + dot(head_t[low:high], right_tail)
                    + dot(tail_t[low:high], right)
                )
                for b in bands:
                    for jj in range(j, TILES):
                        gram[h, m * PER_CYCLE + BLOCKS.index((b, jj))] = part[
                            b * BAND_PAD - low : (b + 1) * BAND_PAD - low,
                            (jj - j) * LANES : (jj - j + 1) * LANES,
                        ]

    def up_copy(p):
        return pltpu.make_async_remote_copy(
            src_ref=gram.at[far, p], dst_ref=up_buf.at[p], send_sem=up_send, recv_sem=up_recv.at[p],
            device_id=above, device_id_type=MESH,
        )

    def dn_copy(p):
        return pltpu.make_async_remote_copy(
            src_ref=gram.at[near, p], dst_ref=dn_buf.at[p], send_sem=dn_send, recv_sem=dn_recv.at[p],
            device_id=below, device_id_type=MESH,
        )

    def hand_out(m, b):
        return pltpu.make_async_remote_copy(
            src_ref=full.at[m, b], dst_ref=fin.at[m], send_sem=fin_send.at[m], recv_sem=fin_recv.at[m],
            device_id={"pix": pix, "train": b}, device_id_type=MESH,
        )

    up_lag = s * LAG
    dn_lag = jnp.where(s == 0, HALF * LAG, (HALF - 1 - s) * LAG)

    def advance(step):
        p = step - up_lag

        @pl.when((p >= 0) & (p < PIECES))
        def _():
            @pl.when(s > 0)
            def _():
                up_copy(p).wait_recv()
                gram[far, p] = gram[far, p] + up_buf[p]

            up_copy(p).start()

        q = step - dn_lag

        @pl.when((q >= 0) & (q < PIECES))
        def _():
            @pl.when(s > 0)
            def _():
                @pl.when(s < HALF - 1)
                def _():
                    dn_copy(q).wait_recv()
                    gram[near, q] = gram[near, q] + dn_buf[q]

                dn_copy(q).start()

            @pl.when(s == 0)
            def _():
                up_copy(q).wait_recv()
                dn_copy(q).wait_recv()
                gram[near, q] = gram[near, q] + (up_buf[q] + dn_buf[q])

                @pl.when(q % PER_CYCLE == PER_CYCLE - 1)
                def _():
                    m = q // PER_CYCLE

                    def block(b, j):
                        return gram[near, m * PER_CYCLE + BLOCKS.index((b, j))]

                    for b, j in BLOCKS:
                        full[m, b, j] = block(b, j)
                    first = jnp.concatenate(
                        [
                            jnp.concatenate([block(0, j), block(1, j), block(2, j)[:32]], 0).T
                            for j in (1, 2)
                        ],
                        0,
                    )
                    for b in range(3, BANDS):
                        full[m, b, 0] = first[b * BAND_PAD - LANES : (b + 1) * BAND_PAD - LANES]
                    second = jnp.concatenate(
                        [block(2, 2)[32:], block(3, 2), block(4, 2), block(5, 2)[:16]], 0
                    ).T
                    for b in range(6, BANDS):
                        low = b * BAND_PAD - 2 * LANES
                        full[m, b, 1] = second[low : low + BAND_PAD]

                    @pl.loop(1, BANDS)
                    def _(i):
                        hand_out(m, (t + i) % BANDS).start()

    @pl.loop(0, CYCLE_DEV)
    def _(m):
        partial_grams(m)

        @pl.loop(m * PER_CYCLE, (m + 1) * PER_CYCLE)
        def _(step):
            advance(step)

    @pl.loop(PIECES, PIECES + HALF * LAG)
    def _(step):
        advance(step)

    @pl.loop(0, CYCLE_DEV)
    def _(m):
        @pl.when(s > 0)
        def _():
            hand_out(m, 0).wait_recv()
            for j in range(TILES):
                out[m, :, j * LANES : (j + 1) * LANES] = fin[m, j]

        @pl.when(s == 0)
        def _():
            for j in range(TILES):
                out[m, :, j * LANES : (j + 1) * LANES] = full[m, t, j]
            sent = full.at[m, pl.ds(0, BANDS - 1)]
            pltpu.make_async_copy(sent, sent, fin_send.at[m]).wait()

        others = send.at[m, pl.ds(0, PEERS - 1)]
        pltpu.make_async_copy(others, others, swap_send.at[m]).wait()

    pltpu.make_async_copy(up_buf, up_buf, up_send).wait()

    @pl.when(s > 0)
    def _():
        pltpu.make_async_copy(dn_buf, dn_buf, dn_send).wait()


def summed_bands(send):
    piece = (BAND_PAD, LANES)
    return pl.pallas_call(
        kernel,
        out_shape=jax.ShapeDtypeStruct((CYCLE_DEV, BAND_PAD, TILES * LANES), jnp.float32),
        in_specs=[pl.BlockSpec(memory_space=pltpu.VMEM)],
        out_specs=pl.BlockSpec(memory_space=pltpu.VMEM),
        scratch_shapes=[
            pltpu.VMEM((CYCLE_DEV, PEERS, 2, ROWS, TILES * LANES), jnp.float32),
            pltpu.VMEM((2, PIECES) + piece, jnp.float32),
            pltpu.VMEM((PIECES,) + piece, jnp.float32),
            pltpu.VMEM((PIECES,) + piece, jnp.float32),
            pltpu.VMEM((CYCLE_DEV, BANDS, TILES) + piece, jnp.float32),
            pltpu.VMEM((CYCLE_DEV, TILES) + piece, jnp.float32),
            pltpu.SemaphoreType.DMA((CYCLE_DEV,)),
            pltpu.SemaphoreType.DMA((CYCLE_DEV,)),
            pltpu.SemaphoreType.DMA((CYCLE_DEV,)),
            pltpu.SemaphoreType.DMA,
            pltpu.SemaphoreType.DMA,
            pltpu.SemaphoreType.DMA((PIECES,)),
            pltpu.SemaphoreType.DMA((PIECES,)),
            pltpu.SemaphoreType.DMA((CYCLE_DEV,)),
            pltpu.SemaphoreType.DMA((CYCLE_DEV,)),
        ],
        compiler_params=pltpu.CompilerParams(collective_id=0, has_side_effects=True),
        name="plane_gram",
    )(send)


def prepare_kernel(raw, section, dark, gain, label, cycle_slot, send, banded):
    trains, pulses, pixels = raw.shape
    cycles = cycle_slot.shape[1]
    band = pulses // BANDS
    f32, bf16 = jnp.float32, jnp.bfloat16

    place = lax.broadcasted_iota(jnp.int32, (cycles, cycles), 0)
    slot = 12 * ((place >> 1) & 7) + 96 * (place & 1) + 3 * ((place >> 4) & 3) + (place >> 6)
    cycle = lax.broadcasted_iota(jnp.int32, (cycles, cycles), 1)
    cycle = jnp.sum(jnp.where(slot == cycle_slot[...], cycle, 0), axis=1, keepdims=True)
    member = (cycle == label[...]).astype(f32)
    before = lax.broadcasted_iota(jnp.int32, (pixels, pixels), 0)
    before = (before < lax.broadcasted_iota(jnp.int32, (pixels, pixels), 1)).astype(bf16)
    earlier = jnp.dot(member.astype(bf16), before, preferred_element_type=f32)
    chosen = jnp.concatenate(
        [jnp.where(earlier == w, member, 0.0).astype(bf16) for w in range(DEPTH)], 0
    )

    edge = lax.broadcasted_iota(jnp.int32, (BAND_PAD - band, pixels), 0)
    for b in range(BANDS):
        banded[b * BAND_PAD + band : (b + 1) * BAND_PAD] = jnp.where(edge == 0, 1.0, 0.0)
    for t in range(trains):
        zero, one = section[t] == 0, section[t] == 1
        offset = jnp.where(
            zero, dark[0].astype(f32), jnp.where(one, dark[1].astype(f32), dark[2].astype(f32))
        )
        factor = jnp.where(zero, gain[0:1], jnp.where(one, gain[1:2], gain[2:3]))
        intensity = (raw[t].astype(f32) - offset) * factor
        for b in range(BANDS):
            banded[b * BAND_PAD : b * BAND_PAD + band] = intensity[b * band : (b + 1) * band]
        values = banded[...]
        total = None
        for _ in range(3):
            head = values.astype(bf16)
            values = values - head.astype(f32)
            part = lax.dot_general(
                chosen, head, (((1,), (1,)), ((), ())), preferred_element_type=f32
            )
            total = part if total is None else total + part
        for w in range(DEPTH):
            send[:, w * trains + t, :] = total[w * cycles : (w + 1) * cycles]
    if ROWS > DEPTH * trains:
        send[:, DEPTH * trains :, :] = jnp.zeros((cycles, ROWS - DEPTH * trains, TILES * LANES), f32)


def finish_kernel(total, out):
    band = out.shape[1]
    for m in range(CYCLE_DEV):
        gram = total[m]
        ratio = gram[band : band + 1, band : band + 1] * gram
        ratio = ratio / (gram[:, band : band + 1] * gram[band : band + 1, :])
        for b in range(BANDS):
            out[m, :, b * band : (b + 1) * band] = ratio[:band, b * BAND_PAD : b * BAND_PAD + band]


def on_device(raw_frames, gain_section, dark_offset, rel_gain, cycle_label, cycle_slot):
    trains, pulses, pixels = raw_frames.shape
    cycles = cycle_slot.shape[0]
    vmem = pl.BlockSpec(memory_space=pltpu.VMEM)
    rows = pl.pallas_call(
        prepare_kernel,
        out_shape=jax.ShapeDtypeStruct((cycles, ROWS, TILES * LANES), jnp.float32),
        in_specs=[vmem] * 6,
        out_specs=vmem,
        scratch_shapes=[pltpu.VMEM((BANDS * BAND_PAD, pixels), jnp.float32)],
        name="prepare",
    )(
        raw_frames, gain_section, dark_offset, rel_gain, cycle_label.reshape(1, pixels),
        cycle_slot.reshape(1, cycles),
    )
    rows = rows.reshape(CYCLE_DEV, PEERS, 2, ROWS, TILES * LANES)
    return pl.pallas_call(
        finish_kernel,
        out_shape=jax.ShapeDtypeStruct((CYCLE_DEV, pulses // BANDS, pulses), jnp.float32),
        in_specs=[vmem],
        out_specs=vmem,
        name="finish",
    )(summed_bands(rows))


def solution(mesh):
    placed = (
        P("train", None, "pix"),
        P("train", None, "pix"),
        P(None, None, "pix"),
        P(None, "pix"),
        P("pix", None),
        P(),
    )
    return jax.shard_map(
        on_device, mesh=mesh, in_specs=placed, out_specs=P("pix", "train", None), check_vma=False
    )
```

```python
import functools

import jax
import jax.numpy as jnp
from jax import lax
from jax.experimental import pallas as pl
from jax.experimental.pallas import tpu as pltpu
from jax.sharding import PartitionSpec as P

CYCLE_DEV = 3
DEPTH = 2
BAND_PAD = 48
LANES = 128
TILES = 3
BANDS = 8
ROWS = 8
SERIES = 6
PACKED = 40
Y = 4
Z = 16
HALF = Z // 2
PEERS = Y * BANDS
LAG = 7
BLOCKS = [(b, j) for b in range(BANDS) for j in range(BAND_PAD * b // LANES, TILES)]
PER_CYCLE = len(BLOCKS)
PIECES = PER_CYCLE * CYCLE_DEV
MESH = pl.DeviceIdType.MESH


def kernel(
    send, out, recv, gram, up_buf, dn_buf, full, fin,
    own_sem, swap_send, swap_recv, up_send, dn_send, up_recv, dn_recv, fin_send, fin_recv,
):
    pix = lax.axis_index("pix")
    t = lax.axis_index("train")
    z, y = pix // Y, pix % Y
    me = y * BANDS + t
    turn = (z - t + Z) % Z
    s = turn % HALF
    far = jnp.where(turn < HALF, 1, 0)
    near = 1 - far
    above = {"pix": ((z + 1) % Z) * Y + y, "train": t}
    below = {"pix": ((z + Z - 1) % Z) * Y + y, "train": t}

    def peer(d):
        return {"pix": z * Y + d // BANDS, "train": d % BANDS}

    barrier = pltpu.get_barrier_semaphore()

    @pl.loop(1, PEERS)
    def _(i):
        pl.semaphore_signal(barrier, inc=1, device_id=peer((me + i) % PEERS), device_id_type=MESH)

    pl.semaphore_signal(barrier, inc=1, device_id=above, device_id_type=MESH)
    pl.semaphore_signal(barrier, inc=1, device_id=below, device_id_type=MESH)
    pl.semaphore_wait(barrier, PEERS + 1)

    for m in range(CYCLE_DEV):

        @pl.loop(1, PEERS)
        def _(i):
            d = (me + i) % PEERS
            pltpu.make_async_remote_copy(
                src_ref=send.at[m, d], dst_ref=recv.at[m, me],
                send_sem=swap_send.at[m], recv_sem=swap_recv.at[m],
                device_id=peer(d), device_id_type=MESH,
            ).start()

        pltpu.make_async_copy(send.at[m, me], recv.at[m, me], own_sem.at[m]).start()

    def partial_grams(m):
        pltpu.make_async_copy(send.at[m, me], recv.at[m, me], own_sem.at[m]).wait()
        others = recv.at[m, pl.ds(0, PEERS - 1)]
        pltpu.make_async_copy(others, others, swap_recv.at[m]).wait()
        for h in range(2):
            blank = jnp.zeros((PEERS, ROWS - SERIES, LANES), jnp.float32)
            rows = []
            for j in range(TILES):
                first = (2 * j + h) * SERIES
                tile = jnp.concatenate([recv[m, :, first : first + SERIES], blank], 1)
                rows.append(tile.reshape(PEERS * ROWS, LANES))
            rows = jnp.concatenate(rows, 1)
            head = rows.astype(jnp.bfloat16)
            tail = (rows - head.astype(jnp.float32)).astype(jnp.bfloat16)
            turned = rows.T
            head_t = turned.astype(jnp.bfloat16)
            tail_t = (turned - head_t.astype(jnp.float32)).astype(jnp.bfloat16)
            for j in range(TILES):
                bands = [b for b in range(BANDS) if BAND_PAD * b // LANES == j]
                low, high = bands[0] * BAND_PAD, (bands[-1] + 1) * BAND_PAD
                dot = functools.partial(jnp.dot, preferred_element_type=jnp.float32)
                right, right_tail = head[:, j * LANES :], tail[:, j * LANES :]
                part = (
                    dot(head_t[low:high], right)
                    + dot(head_t[low:high], right_tail)
                    + dot(tail_t[low:high], right)
                )
                for b in bands:
                    for jj in range(j, TILES):
                        gram[h, m * PER_CYCLE + BLOCKS.index((b, jj))] = part[
                            b * BAND_PAD - low : (b + 1) * BAND_PAD - low,
                            (jj - j) * LANES : (jj - j + 1) * LANES,
                        ]

    def up_copy(p):
        return pltpu.make_async_remote_copy(
            src_ref=gram.at[far, p], dst_ref=up_buf.at[p], send_sem=up_send, recv_sem=up_recv.at[p],
            device_id=above, device_id_type=MESH,
        )

    def dn_copy(p):
        return pltpu.make_async_remote_copy(
            src_ref=gram.at[near, p], dst_ref=dn_buf.at[p], send_sem=dn_send, recv_sem=dn_recv.at[p],
            device_id=below, device_id_type=MESH,
        )

    def hand_out(m, b):
        return pltpu.make_async_remote_copy(
            src_ref=full.at[m, b], dst_ref=fin.at[m], send_sem=fin_send.at[m], recv_sem=fin_recv.at[m],
            device_id={"pix": pix, "train": b}, device_id_type=MESH,
        )

    up_lag = s * LAG
    dn_lag = jnp.where(s == 0, HALF * LAG, (HALF - 1 - s) * LAG)

    def advance(step):
        p = step - up_lag

        @pl.when((p >= 0) & (p < PIECES))
        def _():
            @pl.when(s > 0)
            def _():
                up_copy(p).wait_recv()
                gram[far, p] = gram[far, p] + up_buf[p]

            up_copy(p).start()

        q = step - dn_lag

        @pl.when((q >= 0) & (q < PIECES))
        def _():
            @pl.when(s > 0)
            def _():
                @pl.when(s < HALF - 1)
                def _():
                    dn_copy(q).wait_recv()
                    gram[near, q] = gram[near, q] + dn_buf[q]

                dn_copy(q).start()

            @pl.when(s == 0)
            def _():
                up_copy(q).wait_recv()
                dn_copy(q).wait_recv()
                gram[near, q] = gram[near, q] + (up_buf[q] + dn_buf[q])

                @pl.when(q % PER_CYCLE == PER_CYCLE - 1)
                def _():
                    m = q // PER_CYCLE

                    def block(b, j):
                        return gram[near, m * PER_CYCLE + BLOCKS.index((b, j))]

                    for b, j in BLOCKS:
                        full[m, b, j] = block(b, j)
                    first = jnp.concatenate(
                        [
                            jnp.concatenate([block(0, j), block(1, j), block(2, j)[:32]], 0).T
                            for j in (1, 2)
                        ],
                        0,
                    )
                    for b in range(3, BANDS):
                        full[m, b, 0] = first[b * BAND_PAD - LANES : (b + 1) * BAND_PAD - LANES]
                    second = jnp.concatenate(
                        [block(2, 2)[32:], block(3, 2), block(4, 2), block(5, 2)[:16]], 0
                    ).T
                    for b in range(6, BANDS):
                        low = b * BAND_PAD - 2 * LANES
                        full[m, b, 1] = second[low : low + BAND_PAD]

                    @pl.loop(1, BANDS)
                    def _(i):
                        hand_out(m, (t + i) % BANDS).start()

    @pl.loop(0, CYCLE_DEV)
    def _(m):
        partial_grams(m)

        @pl.loop(m * PER_CYCLE, (m + 1) * PER_CYCLE)
        def _(step):
            advance(step)

    @pl.loop(PIECES, PIECES + HALF * LAG)
    def _(step):
        advance(step)

    @pl.loop(0, CYCLE_DEV)
    def _(m):
        @pl.when(s > 0)
        def _():
            hand_out(m, 0).wait_recv()
            for j in range(TILES):
                out[m, :, j * LANES : (j + 1) * LANES] = fin[m, j]

        @pl.when(s == 0)
        def _():
            for j in range(TILES):
                out[m, :, j * LANES : (j + 1) * LANES] = full[m, t, j]
            sent = full.at[m, pl.ds(0, BANDS - 1)]
            pltpu.make_async_copy(sent, sent, fin_send.at[m]).wait()

        others = send.at[m, pl.ds(0, PEERS - 1)]
        pltpu.make_async_copy(others, others, swap_send.at[m]).wait()

    pltpu.make_async_copy(up_buf, up_buf, up_send).wait()

    @pl.when(s > 0)
    def _():
        pltpu.make_async_copy(dn_buf, dn_buf, dn_send).wait()


def summed_bands(send):
    piece = (BAND_PAD, LANES)
    return pl.pallas_call(
        kernel,
        out_shape=jax.ShapeDtypeStruct((CYCLE_DEV, BAND_PAD, TILES * LANES), jnp.float32),
        in_specs=[pl.BlockSpec(memory_space=pltpu.VMEM)],
        out_specs=pl.BlockSpec(memory_space=pltpu.VMEM),
        scratch_shapes=[
            pltpu.VMEM((CYCLE_DEV, PEERS, PACKED, LANES), jnp.float32),
            pltpu.VMEM((2, PIECES) + piece, jnp.float32),
            pltpu.VMEM((PIECES,) + piece, jnp.float32),
            pltpu.VMEM((PIECES,) + piece, jnp.float32),
            pltpu.VMEM((CYCLE_DEV, BANDS, TILES) + piece, jnp.float32),
            pltpu.VMEM((CYCLE_DEV, TILES) + piece, jnp.float32),
            pltpu.SemaphoreType.DMA((CYCLE_DEV,)),
            pltpu.SemaphoreType.DMA((CYCLE_DEV,)),
            pltpu.SemaphoreType.DMA((CYCLE_DEV,)),
            pltpu.SemaphoreType.DMA,
            pltpu.SemaphoreType.DMA,
            pltpu.SemaphoreType.DMA((PIECES,)),
            pltpu.SemaphoreType.DMA((PIECES,)),
            pltpu.SemaphoreType.DMA((CYCLE_DEV,)),
            pltpu.SemaphoreType.DMA((CYCLE_DEV,)),
        ],
        compiler_params=pltpu.CompilerParams(collective_id=0, has_side_effects=True),
        name="plane_gram",
    )(send)


def prepare_kernel(raw, section, dark, gain, label, cycle_slot, send, banded):
    trains, pulses, pixels = raw.shape
    cycles = cycle_slot.shape[1]
    band = pulses // BANDS
    f32, bf16 = jnp.float32, jnp.bfloat16

    place = lax.broadcasted_iota(jnp.int32, (cycles, cycles), 0)
    half = (place >= cycles // 2).astype(jnp.int32)
    place = place - half * (cycles // 2)
    slot = 12 * (place & 7) + 96 * half + 3 * ((place >> 3) & 3) + (place >> 5)
    cycle = lax.broadcasted_iota(jnp.int32, (cycles, cycles), 1)
    cycle = jnp.sum(jnp.where(slot == cycle_slot[...], cycle, 0), axis=1, keepdims=True)
    member = (cycle == label[...]).astype(f32)
    before = lax.broadcasted_iota(jnp.int32, (pixels, pixels), 0)
    before = (before < lax.broadcasted_iota(jnp.int32, (pixels, pixels), 1)).astype(bf16)
    earlier = jnp.dot(member.astype(bf16), before, preferred_element_type=f32)
    chosen = jnp.concatenate(
        [jnp.where(earlier == w, member, 0.0).astype(bf16) for w in range(DEPTH)], 0
    )

    edge = lax.broadcasted_iota(jnp.int32, (BAND_PAD - band, pixels), 0)
    for b in range(BANDS):
        banded[b * BAND_PAD + band : (b + 1) * BAND_PAD] = jnp.where(edge == 0, 1.0, 0.0)
    for t in range(trains):
        zero, one = section[t] == 0, section[t] == 1
        offset = jnp.where(
            zero, dark[0].astype(f32), jnp.where(one, dark[1].astype(f32), dark[2].astype(f32))
        )
        factor = jnp.where(zero, gain[0:1], jnp.where(one, gain[1:2], gain[2:3]))
        intensity = (raw[t].astype(f32) - offset) * factor
        for b in range(BANDS):
            banded[b * BAND_PAD : b * BAND_PAD + band] = intensity[b * band : (b + 1) * band]
        values = banded[...]
        total = None
        for _ in range(3):
            head = values.astype(bf16)
            values = values - head.astype(f32)
            part = lax.dot_general(
                chosen, head, (((1,), (1,)), ((), ())), preferred_element_type=f32
            )
            total = part if total is None else total + part
        for w in range(DEPTH):
            for h in range(2):
                low = w * cycles + h * (cycles // 2)
                for j in range(TILES):
                    send[:, (2 * j + h) * SERIES + w * trains + t, :] = total[
                        low : low + cycles // 2, j * LANES : (j + 1) * LANES
                    ]
    used = 2 * TILES * SERIES
    send[:, used:, :] = jnp.zeros((cycles // 2, PACKED - used, LANES), f32)


def finish_kernel(total, out):
    band = out.shape[1]
    for m in range(CYCLE_DEV):
        gram = total[m]
        ratio = gram[band : band + 1, band : band + 1] * gram
        ratio = ratio / (gram[:, band : band + 1] * gram[band : band + 1, :])
        for b in range(BANDS):
            out[m, :, b * band : (b + 1) * band] = ratio[:band, b * BAND_PAD : b * BAND_PAD + band]


def on_device(raw_frames, gain_section, dark_offset, rel_gain, cycle_label, cycle_slot):
    trains, pulses, pixels = raw_frames.shape
    cycles = cycle_slot.shape[0]
    vmem = pl.BlockSpec(memory_space=pltpu.VMEM)
    rows = pl.pallas_call(
        prepare_kernel,
        out_shape=jax.ShapeDtypeStruct((cycles // 2, PACKED, LANES), jnp.float32),
        in_specs=[vmem] * 6,
        out_specs=vmem,
        scratch_shapes=[pltpu.VMEM((BANDS * BAND_PAD, pixels), jnp.float32)],
        name="prepare",
    )(
        raw_frames, gain_section, dark_offset, rel_gain, cycle_label.reshape(1, pixels),
        cycle_slot.reshape(1, cycles),
    )
    rows = rows.reshape(CYCLE_DEV, PEERS, PACKED, LANES)
    return pl.pallas_call(
        finish_kernel,
        out_shape=jax.ShapeDtypeStruct((CYCLE_DEV, pulses // BANDS, pulses), jnp.float32),
        in_specs=[vmem],
        out_specs=vmem,
        name="finish",
    )(summed_bands(rows))


def solution(mesh):
    placed = (
        P("train", None, "pix"),
        P("train", None, "pix"),
        P(None, None, "pix"),
        P(None, "pix"),
        P("pix", None),
        P(),
    )
    return jax.shard_map(
        on_device, mesh=mesh, in_specs=placed, out_specs=P("pix", "train", None), check_vma=False
    )
```

```python
import functools

import jax
import jax.numpy as jnp
from jax import lax
from jax.experimental import pallas as pl
from jax.experimental.pallas import tpu as pltpu
from jax.sharding import PartitionSpec as P

CYCLE_DEV = 3
DEPTH = 2
BAND_PAD = 48
LANES = 128
TILES = 3
BANDS = 8
ROWS = 8
SERIES = 6
PACKED = 40
Y = 4
Z = 16
HALF = Z // 2
PEERS = Y * BANDS
LAG = 13
BLOCKS = [(b, j) for b in range(BANDS) for j in range(BAND_PAD * b // LANES, TILES)]
PER_CYCLE = 2 * len(BLOCKS)
PIECE_ROWS = BAND_PAD // 2
PIECES = PER_CYCLE * CYCLE_DEV
MESH = pl.DeviceIdType.MESH


def kernel(
    send, out, recv, gram, up_buf, dn_buf, full, fin,
    own_sem, swap_send, swap_recv, up_send, dn_send, up_recv, dn_recv, fin_send, fin_recv,
):
    pix = lax.axis_index("pix")
    t = lax.axis_index("train")
    z, y = pix // Y, pix % Y
    me = y * BANDS + t
    turn = (z - t + Z) % Z
    s = turn % HALF
    far = jnp.where(turn < HALF, 1, 0)
    near = 1 - far
    above = {"pix": ((z + 1) % Z) * Y + y, "train": t}
    below = {"pix": ((z + Z - 1) % Z) * Y + y, "train": t}

    def peer(d):
        return {"pix": z * Y + d // BANDS, "train": d % BANDS}

    barrier = pltpu.get_barrier_semaphore()

    @pl.loop(1, PEERS)
    def _(i):
        pl.semaphore_signal(barrier, inc=1, device_id=peer((me + i) % PEERS), device_id_type=MESH)

    pl.semaphore_signal(barrier, inc=1, device_id=above, device_id_type=MESH)
    pl.semaphore_signal(barrier, inc=1, device_id=below, device_id_type=MESH)
    pl.semaphore_wait(barrier, PEERS + 1)

    for m in range(CYCLE_DEV):

        @pl.loop(1, PEERS)
        def _(i):
            d = (me + i) % PEERS
            pltpu.make_async_remote_copy(
                src_ref=send.at[m, d], dst_ref=recv.at[m, me],
                send_sem=swap_send.at[m], recv_sem=swap_recv.at[m],
                device_id=peer(d), device_id_type=MESH,
            ).start()

        pltpu.make_async_copy(send.at[m, me], recv.at[m, me], own_sem.at[m]).start()

    def partial_grams(m):
        pltpu.make_async_copy(send.at[m, me], recv.at[m, me], own_sem.at[m]).wait()
        others = recv.at[m, pl.ds(0, PEERS - 1)]
        pltpu.make_async_copy(others, others, swap_recv.at[m]).wait()
        for h in range(2):
            blank = jnp.zeros((PEERS, ROWS - SERIES, LANES), jnp.float32)
            rows = []
            for j in range(TILES):
                first = (2 * j + h) * SERIES
                tile = jnp.concatenate([recv[m, :, first : first + SERIES], blank], 1)
                rows.append(tile.reshape(PEERS * ROWS, LANES))
            rows = jnp.concatenate(rows, 1)
            head = rows.astype(jnp.bfloat16)
            tail = (rows - head.astype(jnp.float32)).astype(jnp.bfloat16)
            turned = rows.T
            head_t = turned.astype(jnp.bfloat16)
            tail_t = (turned - head_t.astype(jnp.float32)).astype(jnp.bfloat16)
            for j in range(TILES):
                bands = [b for b in range(BANDS) if BAND_PAD * b // LANES == j]
                low, high = bands[0] * BAND_PAD, (bands[-1] + 1) * BAND_PAD
                dot = functools.partial(jnp.dot, preferred_element_type=jnp.float32)
                right, right_tail = head[:, j * LANES :], tail[:, j * LANES :]
                part = (
                    dot(head_t[low:high], right)
                    + dot(head_t[low:high], right_tail)
                    + dot(tail_t[low:high], right)
                )
                for b in bands:
                    for jj in range(j, TILES):
                        for e in range(2):
                            top = b * BAND_PAD - low + e * PIECE_ROWS
                            gram[h, m * PER_CYCLE + 2 * BLOCKS.index((b, jj)) + e] = part[
                                top : top + PIECE_ROWS, (jj - j) * LANES : (jj - j + 1) * LANES
                            ]

    def up_copy(p):
        return pltpu.make_async_remote_copy(
            src_ref=gram.at[far, p], dst_ref=up_buf.at[p], send_sem=up_send, recv_sem=up_recv.at[p],
            device_id=above, device_id_type=MESH,
        )

    def dn_copy(p):
        return pltpu.make_async_remote_copy(
            src_ref=gram.at[near, p], dst_ref=dn_buf.at[p], send_sem=dn_send, recv_sem=dn_recv.at[p],
            device_id=below, device_id_type=MESH,
        )

    def hand_out(m, b):
        return pltpu.make_async_remote_copy(
            src_ref=full.at[m, b], dst_ref=fin.at[m], send_sem=fin_send.at[m], recv_sem=fin_recv.at[m],
            device_id={"pix": pix, "train": b}, device_id_type=MESH,
        )

    up_lag = s * LAG
    dn_lag = jnp.where(s == 0, HALF * LAG, (HALF - 1 - s) * LAG)

    def advance(step):
        p = step - up_lag

        @pl.when((p >= 0) & (p < PIECES))
        def _():
            @pl.when(s > 0)
            def _():
                up_copy(p).wait_recv()
                gram[far, p] = gram[far, p] + up_buf[p]

            up_copy(p).start()

        q = step - dn_lag

        @pl.when((q >= 0) & (q < PIECES))
        def _():
            @pl.when(s > 0)
            def _():
                @pl.when(s < HALF - 1)
                def _():
                    dn_copy(q).wait_recv()
                    gram[near, q] = gram[near, q] + dn_buf[q]

                dn_copy(q).start()

            @pl.when(s == 0)
            def _():
                up_copy(q).wait_recv()
                dn_copy(q).wait_recv()
                gram[near, q] = gram[near, q] + (up_buf[q] + dn_buf[q])

                @pl.when(q % PER_CYCLE == PER_CYCLE - 1)
                def _():
                    m = q // PER_CYCLE

                    def block(b, j):
                        first = m * PER_CYCLE + 2 * BLOCKS.index((b, j))
                        return jnp.concatenate([gram[near, first], gram[near, first + 1]], 0)

                    for b, j in BLOCKS:
                        full[m, b, j] = block(b, j)
                    first = jnp.concatenate(
                        [
                            jnp.concatenate([block(0, j), block(1, j), block(2, j)[:32]], 0).T
                            for j in (1, 2)
                        ],
                        0,
                    )
                    for b in range(3, BANDS):
                        full[m, b, 0] = first[b * BAND_PAD - LANES : (b + 1) * BAND_PAD - LANES]
                    second = jnp.concatenate(
                        [block(2, 2)[32:], block(3, 2), block(4, 2), block(5, 2)[:16]], 0
                    ).T
                    for b in range(6, BANDS):
                        low = b * BAND_PAD - 2 * LANES
                        full[m, b, 1] = second[low : low + BAND_PAD]

                    @pl.loop(1, BANDS)
                    def _(i):
                        hand_out(m, (t + i) % BANDS).start()

    @pl.loop(0, CYCLE_DEV)
    def _(m):
        partial_grams(m)

        @pl.loop(m * PER_CYCLE, (m + 1) * PER_CYCLE)
        def _(step):
            advance(step)

    @pl.loop(PIECES, PIECES + HALF * LAG)
    def _(step):
        advance(step)

    @pl.loop(0, CYCLE_DEV)
    def _(m):
        @pl.when(s > 0)
        def _():
            hand_out(m, 0).wait_recv()
            for j in range(TILES):
                out[m, :, j * LANES : (j + 1) * LANES] = fin[m, j]

        @pl.when(s == 0)
        def _():
            for j in range(TILES):
                out[m, :, j * LANES : (j + 1) * LANES] = full[m, t, j]
            sent = full.at[m, pl.ds(0, BANDS - 1)]
            pltpu.make_async_copy(sent, sent, fin_send.at[m]).wait()

        others = send.at[m, pl.ds(0, PEERS - 1)]
        pltpu.make_async_copy(others, others, swap_send.at[m]).wait()

    pltpu.make_async_copy(up_buf, up_buf, up_send).wait()

    @pl.when(s > 0)
    def _():
        pltpu.make_async_copy(dn_buf, dn_buf, dn_send).wait()


def summed_bands(send):
    piece = (BAND_PAD, LANES)
    return pl.pallas_call(
        kernel,
        out_shape=jax.ShapeDtypeStruct((CYCLE_DEV, BAND_PAD, TILES * LANES), jnp.float32),
        in_specs=[pl.BlockSpec(memory_space=pltpu.VMEM)],
        out_specs=pl.BlockSpec(memory_space=pltpu.VMEM),
        scratch_shapes=[
            pltpu.VMEM((CYCLE_DEV, PEERS, PACKED, LANES), jnp.float32),
            pltpu.VMEM((2, PIECES, PIECE_ROWS, LANES), jnp.float32),
            pltpu.VMEM((PIECES, PIECE_ROWS, LANES), jnp.float32),
            pltpu.VMEM((PIECES, PIECE_ROWS, LANES), jnp.float32),
            pltpu.VMEM((CYCLE_DEV, BANDS, TILES) + piece, jnp.float32),
            pltpu.VMEM((CYCLE_DEV, TILES) + piece, jnp.float32),
            pltpu.SemaphoreType.DMA((CYCLE_DEV,)),
            pltpu.SemaphoreType.DMA((CYCLE_DEV,)),
            pltpu.SemaphoreType.DMA((CYCLE_DEV,)),
            pltpu.SemaphoreType.DMA,
            pltpu.SemaphoreType.DMA,
            pltpu.SemaphoreType.DMA((PIECES,)),
            pltpu.SemaphoreType.DMA((PIECES,)),
            pltpu.SemaphoreType.DMA((CYCLE_DEV,)),
            pltpu.SemaphoreType.DMA((CYCLE_DEV,)),
        ],
        compiler_params=pltpu.CompilerParams(collective_id=0, has_side_effects=True),
        name="plane_gram",
    )(send)


def prepare_kernel(raw, section, dark, gain, label, cycle_slot, send, banded):
    trains, pulses, pixels = raw.shape
    cycles = cycle_slot.shape[1]
    band = pulses // BANDS
    f32, bf16 = jnp.float32, jnp.bfloat16

    place = lax.broadcasted_iota(jnp.int32, (cycles, cycles), 0)
    half = (place >= cycles // 2).astype(jnp.int32)
    place = place - half * (cycles // 2)
    slot = 12 * (place & 7) + 96 * half + 3 * ((place >> 3) & 3) + (place >> 5)
    cycle = lax.broadcasted_iota(jnp.int32, (cycles, cycles), 1)
    cycle = jnp.sum(jnp.where(slot == cycle_slot[...], cycle, 0), axis=1, keepdims=True)
    member = (cycle == label[...]).astype(f32)
    before = lax.broadcasted_iota(jnp.int32, (pixels, pixels), 0)
    before = (before < lax.broadcasted_iota(jnp.int32, (pixels, pixels), 1)).astype(bf16)
    earlier = jnp.dot(member.astype(bf16), before, preferred_element_type=f32)
    chosen = jnp.concatenate(
        [jnp.where(earlier == w, member, 0.0).astype(bf16) for w in range(DEPTH)], 0
    )

    edge = lax.broadcasted_iota(jnp.int32, (BAND_PAD - band, pixels), 0)
    for b in range(BANDS):
        banded[b * BAND_PAD + band : (b + 1) * BAND_PAD] = jnp.where(edge == 0, 1.0, 0.0)
    for t in range(trains):
        zero, one = section[t] == 0, section[t] == 1
        offset = jnp.where(
            zero, dark[0].astype(f32), jnp.where(one, dark[1].astype(f32), dark[2].astype(f32))
        )
        factor = jnp.where(zero, gain[0:1], jnp.where(one, gain[1:2], gain[2:3]))
        intensity = (raw[t].astype(f32) - offset) * factor
        for b in range(BANDS):
            banded[b * BAND_PAD : b * BAND_PAD + band] = intensity[b * band : (b + 1) * band]
        values = banded[...]
        total = None
        for _ in range(3):
            head = values.astype(bf16)
            values = values - head.astype(f32)
            part = lax.dot_general(
                chosen, head, (((1,), (1,)), ((), ())), preferred_element_type=f32
            )
            total = part if total is None else total + part
        for w in range(DEPTH):
            for h in range(2):
                low = w * cycles + h * (cycles // 2)
                for j in range(TILES):
                    send[:, (2 * j + h) * SERIES + w * trains + t, :] = total[
                        low : low + cycles // 2, j * LANES : (j + 1) * LANES
                    ]
    used = 2 * TILES * SERIES
    send[:, used:, :] = jnp.zeros((cycles // 2, PACKED - used, LANES), f32)


def finish_kernel(total, out):
    band = out.shape[1]
    for m in range(CYCLE_DEV):
        gram = total[m]
        ratio = gram[band : band + 1, band : band + 1] * gram
        ratio = ratio / (gram[:, band : band + 1] * gram[band : band + 1, :])
        for b in range(BANDS):
            out[m, :, b * band : (b + 1) * band] = ratio[:band, b * BAND_PAD : b * BAND_PAD + band]


def on_device(raw_frames, gain_section, dark_offset, rel_gain, cycle_label, cycle_slot):
    trains, pulses, pixels = raw_frames.shape
    cycles = cycle_slot.shape[0]
    vmem = pl.BlockSpec(memory_space=pltpu.VMEM)
    rows = pl.pallas_call(
        prepare_kernel,
        out_shape=jax.ShapeDtypeStruct((cycles // 2, PACKED, LANES), jnp.float32),
        in_specs=[vmem] * 6,
        out_specs=vmem,
        scratch_shapes=[pltpu.VMEM((BANDS * BAND_PAD, pixels), jnp.float32)],
        name="prepare",
    )(
        raw_frames, gain_section, dark_offset, rel_gain, cycle_label.reshape(1, pixels),
        cycle_slot.reshape(1, cycles),
    )
    rows = rows.reshape(CYCLE_DEV, PEERS, PACKED, LANES)
    return pl.pallas_call(
        finish_kernel,
        out_shape=jax.ShapeDtypeStruct((CYCLE_DEV, pulses // BANDS, pulses), jnp.float32),
        in_specs=[vmem],
        out_specs=vmem,
        name="finish",
    )(summed_bands(rows))


def solution(mesh):
    placed = (
        P("train", None, "pix"),
        P("train", None, "pix"),
        P(None, None, "pix"),
        P(None, "pix"),
        P("pix", None),
        P(),
    )
    return jax.shard_map(
        on_device, mesh=mesh, in_specs=placed, out_specs=P("pix", "train", None), check_vma=False
    )
```
